32 devices in a mesh: grp: 2 (over x), seq: 16 (over z, y, core).
Axes of the slice: x: 2, y: 2, z: 4, core: 2. Of those that a mesh axis runs over, the one named last changes fastest.
Arguments:
- inputs: bfloat16 [4096, 4096], P(('grp', 'seq')), parts along dimension 0, may hold values from -6 to 6
- in_weight: bfloat16 [4096, 768], replicated, may hold values from -0.09375 to 0.09375
- filter_taps: float32 [2048, 256], P('seq'), may hold values from -6 to 6
- grad_out: bfloat16 [4096, 256], P(('grp', 'seq')), parts along dimension 0, may hold values from -6 to 6
Outputs:
- grad_inputs: bfloat16 [4096, 4096], P(('grp', 'seq')), parts along dimension 0
- grad_weight: float32 [8192, 768], P(('grp', 'seq')), parts along dimension 0
- grad_taps: float32 [4096, 256], P(('grp', 'seq')), parts along dimension 0
The draws below stay inside these ranges and needn't reach their ends.
There are 2 independent parts, one for each index of `grp`. The reference program is written for one: setup_inputs(seed, part) draws one part's arguments, and reference() takes and returns one part's arrays. A program takes and returns all parts, laid end to end along the dimension named above; an argument that names none is the same for every part. Nothing has to cross between parts.
All inputs are finite; a program needn't handle non-finite values.
Results may differ from the reference program's by a relative error of at most 0.0064.
Values sent between devices are 32-bit elements; how exact they have to be, the bound alone decides.
A program may use at most 128 MiB of HBM per device.

```python
import math
import jax
import jax.numpy as jnp
from jax import lax

D = 4096
CH = 256
SEQ = 2048


def raised(result, stream_key, source, target, parts, factor):
    def block_of(axis_at):
        return (jnp.arange(result.shape[axis_at]) // (result.shape[axis_at] // parts)).reshape((-1,) + (1,) * (result.ndim - 1 - axis_at))

    first = jax.random.permutation(stream_key, parts)[block_of(target)]
    second = (block_of(target) + parts // 2) % parts
    return jnp.where((block_of(source) == first) | (block_of(source) == second), factor * result, result)


def shard_levels(stream_key, dims, cuts, smallest, high):
    gain = 1.0
    for position, parts in cuts:
        steps = jax.random.uniform(jax.random.fold_in(jax.random.fold_in(stream_key, 6), position), (parts,), jnp.float32, smallest / len(cuts), high / len(cuts))
        gain = gain * jnp.repeat(jnp.exp(steps), dims[position] // parts).reshape((-1,) + (1,) * (len(dims) - 1 - position))
    return gain


def normal_values(own_key, shape, width, limit, split=(), kind=jnp.bfloat16):
    level = shard_levels(own_key, shape, split, -0.22, 0.18) if split else 1.0
    drawn = jax.random.normal(own_key, shape, jnp.float32) * width * level
    return jnp.minimum(jnp.maximum(drawn, -limit), limit).astype(kind)


def heavy_noise(own_key, shape, spread, bound, split, heavy, kind=jnp.bfloat16):
    drawn = spread * jax.random.normal(own_key, shape, jnp.float32)
    if split:
        drawn = drawn * shard_levels(own_key, shape, split, -0.22, 0.18)
    return jnp.clip(raised(drawn, jax.random.fold_in(own_key, 3), *heavy), -bound, bound).astype(kind)


def setup_inputs(seed: int = 0, part: int = 0) -> dict:
    seeds = jax.random.split(jax.random.key(seed), 5)
    part_keys = jax.random.split(jax.random.fold_in(seeds[4], part), 5)
    inputs = heavy_noise(part_keys[0], (SEQ, D), 1.0, 6.0, ((0, 16),), (0, 1, 16, 2.0))
    in_weight = normal_values(seeds[1], (D, 3 * CH), D ** -0.5, 0.09375)
    filter_taps = normal_values(seeds[2], (SEQ, CH), 1.0, 6.0, ((0, 16),), jnp.float32)
    grad_out = normal_values(part_keys[3], (SEQ, CH), 1.0, 6.0, ((0, 16),))
    return {"inputs": inputs, "in_weight": in_weight, "filter_taps": filter_taps, "grad_out": grad_out}


def reference(inputs, in_weight, filter_taps, grad_out):
    seqlen = inputs.shape[0]
    channels = filter_taps.shape[1]
    scaling = 1.0 / math.sqrt(seqlen)
    projected = jnp.dot(inputs, in_weight, preferred_element_type=jnp.float32).astype(jnp.bfloat16)
    query_rows = projected[:, :channels].astype(jnp.float32)
    key_rows = projected[:, channels:2 * channels].astype(jnp.float32)
    value_rows = projected[:, 2 * channels:].astype(jnp.float32)
    gated_input = key_rows * value_rows
    kernel = filter_taps * scaling
    back_grad = grad_out.astype(jnp.float32) * query_rows
    fft_length = 2 * seqlen
    kernel_spec = jnp.fft.rfft(kernel, n=fft_length, axis=0)
    gated_spec = jnp.fft.rfft(gated_input, n=fft_length, axis=0)
    back_spec = jnp.fft.rfft(back_grad, n=fft_length, axis=0)
    mixed_rows = jnp.fft.irfft(kernel_spec * gated_spec, n=fft_length, axis=0)[:seqlen]
    back_conv = jnp.fft.irfft(jnp.conj(kernel_spec) * back_spec, n=fft_length, axis=0)[:seqlen]
    grad_taps = jnp.fft.irfft(back_spec * jnp.conj(gated_spec), n=fft_length, axis=0)[:seqlen] * scaling
    grad_proj = jnp.concatenate([grad_out.astype(jnp.float32) * mixed_rows, back_conv * value_rows, back_conv * key_rows], axis=1).astype(jnp.bfloat16)
    grad_inputs = lax.dot_general(grad_proj, in_weight, (((1,), (1,)), ((), ())), preferred_element_type=jnp.float32).astype(jnp.bfloat16)
    grad_weight = lax.dot_general(inputs, grad_proj, (((0,), (0,)), ((), ())), preferred_element_type=jnp.float32) * scaling
    return (grad_inputs, grad_weight, grad_taps.astype(jnp.float32))
```

```python
import functools
import math

import jax
import jax.numpy as jnp
from jax import lax
from jax.experimental import pallas as pl
from jax.experimental.pallas import tpu as pltpu
from jax.sharding import PartitionSpec as P

GROUP = 16
TEAM = 8
CHIPS = 4
SUBLANES = 8
LANES = 128
PIECES = 4


def round_up(value, step):
    return (value + step - 1) // step * step


def chunks_of(per_device):
    return per_device // SUBLANES if per_device % SUBLANES == 0 else 1


def remote(src, dst, send_sem, recv_sem, peer):
    return pltpu.make_async_remote_copy(
        src_ref=src,
        dst_ref=dst,
        send_sem=send_sem,
        recv_sem=recv_sem,
        device_id={"seq": peer},
        device_id_type=pl.DeviceIdType.MESH,
    )


def fused_kernel(
    n, scaling, x_hbm, weight_hbm, taps_hbm, grad_hbm,
    grad_inputs_ref, out_ref, grad_taps_ref,
    x_ref, taps_ref, grad_ref, weights,
    send_taps, got_taps, send_pair, got_pair, back_rev, conv_rev,
    made_pair, home_pair, made_taps, home_taps,
    pad_gated, pad_back, send_cols, got_cols, left, key_rows, value_rows,
    proj_all, made, got,
    load_sems, weight_sems,
    taps_send, taps_recv, pair_send, pair_recv, home_send, home_recv, last_send, last_recv,
    cols_send, cols_recv, direct_send, relay_send, gather_recv, sums_send, sums_recv,
):
    f32, bf16 = jnp.float32, jnp.bfloat16
    me = lax.axis_index("seq")
    rows, depth = x_ref.shape
    channels = taps_ref.shape[1]
    cpd = channels // n
    chunks = chunks_of(cpd)
    own_channels = cpd // chunks
    slim = round_up(own_channels, SUBLANES)
    wide = channels // chunks
    parts = 3 * chunks
    teams = n // TEAM
    team, mine = me // TEAM, lax.rem(me, TEAM)
    base, chip, core = team * TEAM, mine // 2, lax.rem(mine, 2)
    near = (chip + 1 - 2 * lax.rem(chip, 2)) * 2
    far = lax.rem(chip + 2, CHIPS) * 2
    corner = (CHIPS - 1 - chip) * 2
    sibling = chip * 2 + 1 - core
    block = depth // n
    share = depth // TEAM
    cuts = teams if block % LANES == 0 else 1
    pieces = weight_sems.shape[0]
    piece = depth // pieces

    def slot(ref, index, height):
        return ref.at[pl.ds(pl.multiple_of(index * height, 8), height), :]

    def load(k):
        span = pl.ds(k * piece, piece)
        return pltpu.make_async_copy(
            weight_hbm.at[span, :], weights.at[span, :], weight_sems.at[k]
        )

    small = [
        pltpu.make_async_copy(src, dst, load_sems.at[k])
        for k, (src, dst) in enumerate(
            ((taps_hbm, taps_ref), (x_hbm, x_ref), (grad_hbm, grad_ref))
        )
    ]
    for copy in small:
        copy.start()
    for k in range(pieces):
        load(k).start()
    barrier = pltpu.get_barrier_semaphore()

    @pl.loop(1, n)
    def _(o):
        pl.semaphore_signal(
            barrier, inc=1, device_id={"seq": lax.rem(me + o, n)},
            device_id_type=pl.DeviceIdType.MESH,
        )

    anti = (
        lax.broadcasted_iota(jnp.int32, (rows, rows), 0)
        + lax.broadcasted_iota(jnp.int32, (rows, rows), 1)
        == rows - 1
    )

    def reverse(values):
        return jnp.dot(
            values, anti.astype(f32), preferred_element_type=f32,
            precision=lax.Precision.HIGHEST,
        )

    def turn(values):
        high = values.astype(bf16)
        low = (values - high.astype(f32)).astype(bf16)
        flip = anti.astype(bf16)
        over = (((1,), (1,)), ((), ()))
        return lax.dot_general(
            flip, high, over, preferred_element_type=f32
        ) + lax.dot_general(flip, low, over, preferred_element_type=f32)

    def spread(ref, values, start, step):
        for p in range(n):
            at = start + p * step
            ref[at : at + own_channels, :] = values[p * own_channels : (p + 1) * own_channels, :]

    def collect(ref, start, step):
        return jnp.concatenate(
            [ref[start + p * step : start + p * step + own_channels, :] for p in range(n)], axis=0
        )

    small[0].wait()
    lag_rows = taps_ref[...].T
    for k in range(chunks):
        spread(send_taps, lag_rows[k * wide : (k + 1) * wide], k * slim, chunks * slim)
    small[1].wait()
    for g in range(TEAM):
        for h in range(teams):
            first = (h * TEAM + g) * block
            send_cols[g * rows : (g + 1) * rows, h * block : (h + 1) * block] = x_ref[
                :, first : first + block
            ].astype(f32)
    pl.semaphore_wait(barrier, n - 1)

    def taps_plan(peer, sender):
        return remote(slot(send_taps, peer, chunks * slim), slot(got_taps, sender, chunks * slim),
                      taps_send.at[peer], taps_recv.at[sender], peer)

    def pair_plan(k):
        return lambda peer, sender: remote(
            slot(send_pair, k * n + peer, 2 * slim), slot(got_pair, k * n + sender, 2 * slim),
            pair_send.at[k, peer], pair_recv.at[k, sender], peer)

    def home_plan(k):
        return lambda peer, sender: remote(
            slot(made_pair, k * n + peer, 2 * slim), slot(home_pair, k * n + sender, 2 * slim),
            home_send.at[k, peer], home_recv.at[k, sender], peer)

    def last_plan(peer, sender):
        return remote(slot(made_taps, n - 1 - peer, chunks * slim),
                      slot(home_taps, sender, chunks * slim),
                      last_send.at[peer], last_recv.at[sender], peer)

    def exchange_start(plan):
        @pl.loop(1, n)
        def _(o):
            plan(lax.rem(me + o, n), me).start()

    def exchange_wait(plan, after=None):
        @pl.loop(1, n)
        def _(o):
            other = lax.rem(me + n - o, n)
            plan(other, other).wait_recv()
            if after is not None:
                after(other)

    def exchange_sent(plan):
        @pl.loop(1, n)
        def _(o):
            plan(lax.rem(me + o, n), me).wait_send()

    def cols_cut(ref, member, cut):
        if cuts == 1:
            return slot(ref, member, rows)
        return ref.at[
            pl.ds(pl.multiple_of(member * rows, 8), rows),
            pl.ds(pl.multiple_of(cut * block, LANES), block),
        ]

    def cols(target, sender, peer, cut):
        return remote(cols_cut(send_cols, target, cut), cols_cut(got_cols, sender, cut),
                      cols_send.at[target, cut], cols_recv.at[sender, cut], base + peer)

    def cols_start(other, first, last):
        for o in range(first, last):
            cols(other, mine, other, lax.rem(team + o, cuts) if cuts > 1 else 0).start()

    early = (1, cuts) if cuts > 1 else (0, 1)
    late = (cuts, cuts + 1) if cuts > 1 else (0, 0)

    exchange_start(taps_plan)
    for other in (sibling, near + core, far + core):
        cols_start(other, *early)
    small[2].wait()
    total = jnp.zeros((rows, 3 * channels), f32)
    for k in range(pieces):
        load(k).wait()
        total = total + jnp.dot(
            x_ref[:, k * piece : (k + 1) * piece], weights[k * piece : (k + 1) * piece, :],
            preferred_element_type=f32,
        )
    total = total.astype(bf16).astype(f32)
    key_rows[...] = total[:, channels : 2 * channels]
    value_rows[...] = total[:, 2 * channels :]
    gated = (total[:, channels : 2 * channels] * total[:, 2 * channels :]).T
    back = reverse((grad_ref[...].astype(f32) * total[:, :channels]).T)
    for k in range(chunks):
        spread(send_pair, gated[k * wide : (k + 1) * wide], k * n * 2 * slim, 2 * slim)
        spread(send_pair, back[k * wide : (k + 1) * wide], k * n * 2 * slim + slim, 2 * slim)
        exchange_start(pair_plan(k))
    for other in (near + 1 - core, far + 1 - core, corner + core, corner + 1 - core):
        cols_start(other, *early)

    slot(got_cols, mine, rows)[...] = slot(send_cols, mine, rows)[...]
    slot(got_taps, me, chunks * slim)[...] = slot(send_taps, me, chunks * slim)[...]
    for k in range(chunks):
        slot(got_pair, k * n + me, 2 * slim)[...] = slot(send_pair, k * n + me, 2 * slim)[...]
    unroll = pad_gated.shape[0]
    for u in range(unroll):
        pad_gated[u, pl.ds(0, n), :] = jnp.zeros((n, rows), f32)
        pad_back[u, pl.ds(0, n), :] = jnp.zeros((n, rows), f32)

    lane = lax.broadcasted_iota(jnp.int32, (rows, rows), 1)
    line = lax.broadcasted_iota(jnp.int32, (rows, rows), 0)
    keep = lane >= line
    group = min(GROUP, n)

    def turned(source, index):
        ref, start, step = source
        row = ref[pl.ds(start + index * step, 1), :]
        return pltpu.roll(
            jnp.broadcast_to(row, (rows, rows)), 0, 1, stride=1, stride_axis=0
        )

    def convolve(k, c, u):
        pair_start = k * n * 2 * slim + c
        back_start = k * n * slim + c
        pad_gated[u, pl.ds(n, n), :] = got_pair[pl.ds(pair_start, n, stride=2 * slim), :]
        pad_back[u, pl.ds(n, n), :] = back_rev[pl.ds(back_start, n, stride=slim), :]

        def some_lags(q, total):
            matrices = []
            for source in (
                (got_taps, k * slim + c, chunks * slim), (got_pair, pair_start, 2 * slim)
            ):
                if isinstance(q, int):
                    before = jnp.zeros((rows, rows), f32)
                else:
                    before = turned(source, jnp.maximum(q * group - 1, 0))
                    before = jnp.where(q == 0, 0.0, before)
                tiles = []
                for e in range(group):
                    now = turned(source, q * group + e)
                    tiles.append(jnp.where(keep, now, before).astype(bf16))
                    before = now
                matrices.append(jnp.concatenate(tiles, axis=0))
            table = jnp.concatenate(matrices, axis=1)
            lines = jnp.concatenate(
                [
                    jnp.concatenate(
                        [pad[u, pl.ds(n - q * group - e, n), :] for e in range(group)], axis=1
                    ).astype(bf16)
                    for pad in (pad_gated, pad_back)
                ],
                axis=0,
            )
            return total + jnp.dot(lines, table, preferred_element_type=f32)

        sums = jnp.zeros((2 * n, 2 * rows), f32)
        if n == group:
            sums = some_lags(0, sums)
        else:
            sums = lax.fori_loop(0, n // group, some_lags, sums)
        made_pair[pl.ds(pair_start, n, stride=2 * slim), :] = sums[:n, :rows]
        conv_rev[pl.ds(back_start, n, stride=slim), :] = sums[n:, :rows]
        made_taps[pl.ds(k * slim + c, n, stride=chunks * slim), :] = sums[n:, rows:]

    def back_rows(k, s):
        slot(back_rev, k * n + n - 1 - s, slim)[...] = got_pair[
            pl.ds(pl.multiple_of((k * n + s) * 2 * slim + slim, 8), slim), :
        ]

    exchange_wait(taps_plan)
    for k in range(chunks):
        back_rows(k, me)
        exchange_wait(pair_plan(k), functools.partial(back_rows, k))

        def channel_group(i, carry):
            for u in range(unroll):
                convolve(k, i * unroll + u, u)
            return carry

        lax.fori_loop(0, own_channels // unroll, channel_group, 0)

        @pl.loop(0, n)
        def _(r):
            made_pair[pl.ds(pl.multiple_of((k * n + n - 1 - r) * 2 * slim + slim, 8), slim), :] = (
                slot(conv_rev, k * n + r, slim)[...]
            )

        exchange_start(home_plan(k))
        slot(home_pair, k * n + me, 2 * slim)[...] = slot(made_pair, k * n + me, 2 * slim)[...]
    slot(home_taps, me, chunks * slim)[...] = slot(made_taps, n - 1 - me, chunks * slim)[...]

    def held(part, member):
        return slot(proj_all, part * TEAM + member, rows)

    def pass_on(part, member, sem, peer):
        return remote(held(part, member), held(part, member), sem,
                      gather_recv.at[part, member], base + peer)

    def directs(part):
        return [
            pass_on(part, mine, direct_send.at[part, i], peer)
            for i, peer in enumerate((far + core, near + core, sibling))
        ]

    def relays(part):
        return [
            pass_on(part, far + core, relay_send.at[part, 0], near + core),
            pass_on(part, far + core, relay_send.at[part, 1], sibling),
            pass_on(part, near + core, relay_send.at[part, 2], sibling),
            pass_on(part, corner + core, relay_send.at[part, 3], sibling),
        ]

    def arrived(part, member):
        pass_on(part, member, direct_send.at[part, 0], sibling).wait_recv()

    def project(k):
        exchange_wait(home_plan(k))
        start = k * n * 2 * slim
        mixed = collect(home_pair, start, 2 * slim).T * scaling
        conv = turn(collect(home_pair, start + slim, 2 * slim)) * scaling
        span = slice(k * wide, (k + 1) * wide)
        for j, values in enumerate((
            grad_ref[:, span].astype(f32) * mixed,
            conv * value_rows[:, span],
            conv * key_rows[:, span],
        )):
            held(3 * k + j, mine)[...] = values.astype(bf16).astype(f32)
        for j in range(3):
            for copy in directs(3 * k + j):
                copy.start()

    def cols_wait(first, last):
        @pl.loop(1, TEAM)
        def _(o):
            other = lax.rem(mine + o, TEAM)
            for t in range(first, last):
                cut = lax.rem(team + t, cuts) if cuts > 1 else 0
                cols(other, other, other, cut).wait_recv()

        for t in range(first, last):
            if cuts == 1:
                for s in range(TEAM):
                    left[:, s * rows : (s + 1) * rows] = (
                        got_cols[s * rows : (s + 1) * rows, :].T.astype(bf16)
                    )
            else:
                cut = lax.rem(team + t, cuts)
                for s in range(TEAM):
                    left[pl.ds(pl.multiple_of(cut * block, 16), block), s * rows : (s + 1) * rows] = (
                        got_cols[
                            s * rows : (s + 1) * rows,
                            pl.ds(pl.multiple_of(cut * block, LANES), block),
                        ].T.astype(bf16)
                    )

    def first_relays(k):
        for part in range(3 * k, 3 * k + 3):
            hops = relays(part)
            arrived(part, far + core)
            hops[0].start()
            hops[1].start()
            arrived(part, near + core)
            hops[2].start()

    def second_relays(k):
        for part in range(3 * k, 3 * k + 3):
            arrived(part, corner + core)
            relays(part)[3].start()

    def product(part, index):
        right = proj_all[part * TEAM * rows : (part + 1) * TEAM * rows, :].astype(bf16)
        lines = left[pl.ds(pl.multiple_of(index * block, 16), block), :]
        return jnp.dot(lines, right, preferred_element_type=f32)

    def sums_copy(part, to_team, from_team, peer):
        return remote(slot(made, part * teams + to_team, block),
                      slot(got, part * teams + from_team, block),
                      sums_send.at[part, to_team], sums_recv.at[part, from_team],
                      peer * TEAM + mine)

    def send_sums(k):
        for part in range(3 * k, 3 * k + 3):
            arrived(part, sibling)
            for other in (far + 1 - core, near + 1 - core, corner + 1 - core):
                arrived(part, other)

            def send_one(o, carry):
                target = lax.rem(team + o, teams)
                slot(made, part * teams + target, block)[...] = product(part, target)
                sums_copy(part, target, team, target).start()
                return carry

            lax.fori_loop(1, teams, send_one, 0)

    project(0)
    exchange_start(last_plan)
    for k in range(1, chunks):
        project(k)
    cols_wait(*early)
    for k in range(chunks):
        first_relays(k)
        second_relays(k)
        if k == chunks - 1:
            for other in (sibling, near + core, far + core, near + 1 - core, far + 1 - core,
                          corner + core, corner + 1 - core):
                cols_start(other, *late)
        send_sums(k)

    tile = min(512, depth)
    lines = jnp.concatenate(
        [held(3 * k + j, mine)[...].astype(bf16) for j in range(3) for k in range(chunks)], axis=1
    )

    @pl.loop(0, depth // tile)
    def _(t):
        start = pl.multiple_of(t * tile, tile)
        grad_inputs_ref[:, pl.ds(start, tile)] = lax.dot_general(
            lines, weights[pl.ds(start, tile), :], (((1,), (1,)), ((), ())),
            preferred_element_type=f32,
        ).astype(bf16)

    exchange_wait(last_plan)
    for k in range(chunks):
        grad_taps_ref[:, k * wide : (k + 1) * wide] = (
            turn(collect(home_taps, k * slim, chunks * slim)) * scaling
        )
    cols_wait(*late)

    def columns(part):
        k, j = part // 3, part % 3
        return slice(j * channels + k * wide, j * channels + (k + 1) * wide)

    for part in range(parts):
        out_ref[:, columns(part)] = product(part, team)
    for part in range(parts):
        def add_one(o, carry):
            other = lax.rem(team + o, teams)
            sums_copy(part, other, other, other).wait_recv()
            out_ref[:, columns(part)] = (
                out_ref[:, columns(part)] + slot(got, part * teams + other, block)[...]
            )
            return carry

        lax.fori_loop(1, teams, add_one, 0)
        out_ref[:, columns(part)] = out_ref[:, columns(part)] * scaling

    exchange_sent(taps_plan)
    for k in range(chunks):
        exchange_sent(pair_plan(k))
        exchange_sent(home_plan(k))
    exchange_sent(last_plan)

    @pl.loop(1, TEAM)
    def _(o):
        other = lax.rem(mine + o, TEAM)
        for cut in range(cuts):
            cols(other, mine, other, cut).wait_send()

    for part in range(parts):
        for copy in directs(part) + relays(part):
            copy.wait_send()

        def sent_one(o, carry):
            target = lax.rem(team + o, teams)
            sums_copy(part, target, team, target).wait_send()
            return carry

        lax.fori_loop(1, teams, sent_one, 0)


def write_kernel(*refs):
    sems = refs[-1]
    copies = [pltpu.make_async_copy(refs[k], refs[3 + k], sems.at[k]) for k in range(3)]
    for copy in copies:
        copy.start()
    for copy in copies:
        copy.wait()


def per_device(inputs, in_weight, filter_taps, grad_out):
    rows, depth = inputs.shape
    channels = filter_taps.shape[1]
    n = lax.axis_size("seq")
    scaling = 1.0 / math.sqrt(rows * n)
    cpd = channels // n
    chunks = chunks_of(cpd)
    own_channels = cpd // chunks
    slim = round_up(own_channels, SUBLANES)
    wide = channels // chunks
    parts = 3 * chunks
    teams = n // TEAM
    share = depth // TEAM
    cuts = teams if (depth // n) % LANES == 0 else 1
    unroll = math.gcd(own_channels, 4)
    f32, bf16 = jnp.float32, jnp.bfloat16
    vmem = pl.BlockSpec(memory_space=pltpu.VMEM)
    hbm = pl.BlockSpec(memory_space=pltpu.HBM)
    dma = pltpu.SemaphoreType.DMA
    signal = pltpu.VMEM((n * chunks * slim, rows), f32)
    pair = pltpu.VMEM((2 * n * chunks * slim, rows), f32)
    results = pl.pallas_call(
        functools.partial(fused_kernel, n, scaling),
        out_shape=(
            jax.ShapeDtypeStruct((rows, depth), bf16),
            jax.ShapeDtypeStruct((depth // n, 3 * channels), f32),
            jax.ShapeDtypeStruct((rows, channels), f32),
        ),
        in_specs=[hbm] * 4,
        out_specs=(vmem,) * 3,
        scratch_shapes=[
            pltpu.VMEM(inputs.shape, inputs.dtype),
            pltpu.VMEM(filter_taps.shape, filter_taps.dtype),
            pltpu.VMEM(grad_out.shape, grad_out.dtype),
            pltpu.VMEM(in_weight.shape, in_weight.dtype),
            signal, signal, pair, pair, signal, signal, pair, pair, signal, signal,
            pltpu.VMEM((unroll, 2 * n, rows), f32),
            pltpu.VMEM((unroll, 2 * n, rows), f32),
            pltpu.VMEM((TEAM * rows, share), f32),
            pltpu.VMEM((TEAM * rows, share), f32),
            pltpu.VMEM((share, TEAM * rows), bf16),
            pltpu.VMEM((rows, channels), f32),
            pltpu.VMEM((rows, channels), f32),
            pltpu.VMEM((parts * TEAM * rows, wide), f32),
            pltpu.VMEM((parts * share, wide), f32),
            pltpu.VMEM((parts * share, wide), f32),
            dma((3,)), dma((PIECES,)),
            dma((n,)), dma((n,)), dma((chunks, n)), dma((chunks, n)),
            dma((chunks, n)), dma((chunks, n)), dma((n,)), dma((n,)),
            dma((TEAM, cuts)), dma((TEAM, cuts)),
            dma((parts, 3)), dma((parts, 4)), dma((parts, TEAM)),
            dma((parts, teams)), dma((parts, teams)),
        ],
        compiler_params=pltpu.CompilerParams(
            collective_id=0, has_side_effects=True, vmem_limit_bytes=48 << 20
        ),
    )(*(pltpu.with_memory_space_constraint(a, pltpu.HBM)
        for a in (inputs, in_weight, filter_taps, grad_out)))
    return pl.pallas_call(
        write_kernel,
        out_shape=tuple(jax.ShapeDtypeStruct(r.shape, r.dtype) for r in results),
        in_specs=[vmem] * 3,
        out_specs=(pl.BlockSpec(memory_space=pl.ANY),) * 3,
        scratch_shapes=[dma((3,))],
        compiler_params=pltpu.CompilerParams(vmem_limit_bytes=8 << 20),
    )(*results)


def solution(mesh):
    in_specs = (P(("grp", "seq"), None), P(), P("seq", None), P(("grp", "seq"), None))
    out_specs = (P(("grp", "seq"), None), P(("grp", "seq"), None), P(("grp", "seq"), None))
    return jax.shard_map(
        per_device, mesh=mesh, in_specs=in_specs, out_specs=out_specs, check_vma=False
    )
```
